32 devices in a mesh: tx: 2 (over x), ty: 4 (over z), pg: 4 (over y, core).
Axes of the slice: x: 2, y: 2, z: 4, core: 2. Of those that a mesh axis runs over, the one named last changes fastest.
Arguments:
- direct_modes: bfloat16 [64, 3, 32, 512], P('pg', None, 'tx', 'ty'), may hold values from -6 to 6
- adjoint_modes: bfloat16 [64, 3, 32, 512], P(None, None, 'tx', 'ty'), may hold values from -6 to 6
- block_order: int32 [8], replicated, may hold values from 0 to 7, each once
Outputs:
- tensor: float32 [64, 64, 64], P('pg', 'ty', 'tx')
The draws below stay inside these ranges and needn't reach their ends.
Inputs may be any that keep to these rules, and one draw needn't show every extreme that they name: `block_order`: each of the 8 blocks appears exactly once.
All inputs are finite; a program needn't handle non-finite values.
Results may differ from the reference program's by a relative error of at most 0.0043.
Values may be sent and summed in bfloat16 or wider, within the bound.
A program may use at most 64 MiB of HBM per device.

```python
import math
import jax
import jax.numpy as jnp
from jax import lax

R = 64
K = 64
NBLK = 8
JB = 4
CZ = 4
NX = 32
NY = 128


def block_scale(key, shape, cuts, low, largest):
    def one(axis_at, shards_of):
        heights = jax.random.uniform(jax.random.fold_in(jax.random.fold_in(key, 6), axis_at), (shards_of,), jnp.float32, low / len(cuts), largest / len(cuts))
        return jnp.repeat(jnp.exp(heights), shape[axis_at] // shards_of).reshape((-1,) + (1,) * (len(shape) - axis_at - 1))

    loudness = one(*cuts[0])
    for cut in cuts[1:]:
        loudness = loudness * one(*cut)
    return loudness


def scatter_about(stream_key, shape, scale, reach, cuts=(), held_as=jnp.bfloat16):
    entries = scale * jax.random.normal(stream_key, shape, jnp.float32)
    if cuts:
        entries = entries * block_scale(stream_key, shape, cuts, -0.22, 0.18)
    return jnp.clip(entries, -reach, reach).astype(held_as)


def setup_inputs(seed: int = 0) -> dict:
    splits = jax.random.split(jax.random.key(seed), 4)
    return {
        "direct_modes": scatter_about(splits[0], (R, 3, NX, NY * CZ), 1.0, 6.0, ((0, 4), (2, 2), (3, 4))),
        "adjoint_modes": scatter_about(splits[1], (K, 3, NX, NY * CZ), 1.0, 6.0, ((2, 2), (3, 4))),
        "block_order": jax.random.permutation(splits[2], NBLK).astype(jnp.int32),
    }


def depth_slope(values, depth):
    position = jnp.arange(values.shape[-1]) % depth
    upper = jnp.where(position == depth - 1, jnp.roll(values, depth - 1, -1), jnp.roll(values, -1, -1))
    lower = jnp.where(position == 0, jnp.roll(values, 1 - depth, -1), jnp.roll(values, 1, -1))
    return (upper - lower) * 0.5

def slopes(values, wide_x, wide_y, depth):
    along_x = (wide_x[:, :, 2:] - wide_x[:, :, :-2]) * 0.5
    along_y = (wide_y[..., 2 * depth:] - wide_y[..., :-2 * depth]) * 0.5
    along_z = depth_slope(values, depth)
    return jnp.stack([along_x, along_y, along_z], 1).astype(jnp.bfloat16)

def pair_terms(rows_u, rows_g, cols_u, cols_g):
    result = jnp.zeros((rows_u.shape[0], cols_u.shape[0]) + cols_g.shape[2:], jnp.float32)
    for direction in range(3):
        result = result + rows_u[:, None, direction, None] * cols_g[None, :, direction]
        result = result + cols_u[None, :, direction, None] * rows_g[:, None, direction]
    return result.astype(jnp.bfloat16)

def project(pairs, adjoint):
    flat = pairs.reshape(pairs.shape[0] * pairs.shape[1], -1)
    basis = adjoint.reshape(adjoint.shape[0], -1)
    product = lax.dot_general(flat, basis, (((1,), (1,)), ((), ())), preferred_element_type=jnp.float32)
    return product.reshape(pairs.shape[0], pairs.shape[1], adjoint.shape[0])

def block_tensor(rows_u, rows_g, modes, grads, adjoint, width):
    count = modes.shape[0] // width

    def one_block(start):
        cols_u = lax.dynamic_slice_in_dim(modes, start, width, 0).astype(jnp.float32)
        cols_g = lax.dynamic_slice_in_dim(grads, start, width, 0).astype(jnp.float32)
        return project(pair_terms(rows_u, rows_g, cols_u, cols_g), adjoint)
    starts = (jnp.arange(count) * width).astype(jnp.int32)
    pieces = lax.map(one_block, starts)
    return jnp.transpose(pieces, (1, 0, 2, 3)).reshape(rows_u.shape[0], modes.shape[0], adjoint.shape[0])

def reference(direct_modes, adjoint_modes, block_order):
    values = direct_modes.astype(jnp.float32)
    wide_x = jnp.pad(values, ((0, 0), (0, 0), (1, 1), (0, 0)))
    wide_y = jnp.pad(values, ((0, 0), (0, 0), (0, 0), (CZ, CZ)))
    grads = slopes(values, wide_x, wide_y, CZ)
    block_rows = R // NBLK
    weight = 1.0 / math.sqrt(3.0 * NX * NY * CZ)

    def one_slot(block):
        start = (block * block_rows).astype(jnp.int32)
        rows_u = lax.dynamic_slice_in_dim(direct_modes, start, block_rows, 0).astype(jnp.float32)
        rows_g = lax.dynamic_slice_in_dim(grads, start, block_rows, 0).astype(jnp.float32)
        return block_tensor(rows_u, rows_g, direct_modes, grads, adjoint_modes, JB) * weight
    slots = lax.map(one_slot, block_order)
    return slots.reshape(R, R, K)
```

```python
import functools
import math

import jax
import jax.numpy as jnp
from jax import lax
from jax.experimental import pallas as pl
from jax.experimental.pallas import tpu as pltpu
from jax.sharding import PartitionSpec as P

NBLK = 8
CZ = 4
MESH = pl.DeviceIdType.MESH
F32 = jnp.float32
BF16 = jnp.bfloat16


def kernel(
    tx_n, ty_n, pg_n, weight,
    order_ref, own_ref, adj_ref, out_ref,
    wide, face_lo, face_hi, edge_lo, edge_hi, us, gs, row_us, row_gs, pairs, acc, stage, parts,
    mode_send, mode_recv, x_send, x_recv, y_send, y_recv, part_send, part_recv,
):
    tx, ty, pg = lax.axis_index("tx"), lax.axis_index("ty"), lax.axis_index("pg")
    nx, _, own_n, lanes = own_ref.shape
    group_n = tx_n * ty_n
    me = tx * ty_n + ty
    rows_n = own_n
    blk = pg_n * own_n // NBLK
    per_group = NBLK // pg_n

    has_xl, has_xh = tx > 0, tx < tx_n - 1
    has_yl, has_yh = ty > 0, ty < ty_n - 1

    barrier = pltpu.get_barrier_semaphore()
    for off in range(1, pg_n):
        pl.semaphore_signal(barrier, inc=1, device_id=(tx, ty, lax.rem(pg + off, pg_n)), device_id_type=MESH)
    for off in range(1, group_n):
        to = lax.rem(me + off, group_n)
        pl.semaphore_signal(barrier, inc=1, device_id=(to // ty_n, lax.rem(to, ty_n), pg), device_id_type=MESH)
    for has, dx, dy in ((has_xl, -1, 0), (has_xh, 1, 0), (has_yl, 0, -1), (has_yh, 0, 1)):
        @pl.when(has)
        def _():
            for off in range(1, pg_n):
                pl.semaphore_signal(
                    barrier, inc=1, device_id=(tx + dx, ty + dy, lax.rem(pg + off, pg_n)), device_id_type=MESH)

    lane = lax.broadcasted_iota(jnp.int32, (own_n, lanes), 1)
    for c in range(3):
        low = jnp.zeros((own_n, lanes), F32)
        high = jnp.zeros((own_n, lanes), F32)
        for x in range(nx):
            tile = own_ref[x, c].astype(F32)
            here = (lane >= x * CZ) & (lane < (x + 1) * CZ)
            low = jnp.where(here, pltpu.roll(tile, (x * CZ) % lanes, 1) if x else tile, low)
            high = jnp.where(here, pltpu.roll(tile, (x * CZ + CZ) % lanes, 1), high)
        face_lo[c] = low.astype(BF16)
        face_hi[c] = high.astype(BF16)

    zero = jnp.zeros((pg_n, 3, own_n, lanes), BF16)

    @pl.when(jnp.logical_not(has_xl))
    def _():
        wide[0] = zero

    @pl.when(jnp.logical_not(has_xh))
    def _():
        wide[nx + 1] = zero

    @pl.when(jnp.logical_not(has_yl))
    def _():
        edge_lo[...] = zero

    @pl.when(jnp.logical_not(has_yh))
    def _():
        edge_hi[...] = zero

    neighbours = 1 * (has_xl.astype(jnp.int32) + has_xh.astype(jnp.int32)
                      + has_yl.astype(jnp.int32) + has_yh.astype(jnp.int32))
    pl.semaphore_wait(barrier, (pg_n - 1) + (group_n - 1) + neighbours * (pg_n - 1))

    def mode_copy(off):
        return pltpu.make_async_remote_copy(
            own_ref, wide.at[pl.ds(1, nx), pg], mode_send.at[off], mode_recv.at[off],
            device_id=(tx, ty, lax.rem(pg + off, pg_n)), device_id_type=MESH)

    def x_copy(side, off):
        src, dst, to = (own_ref.at[nx - 1], wide.at[0, pg], tx + 1) if side == 0 else (
            own_ref.at[0], wide.at[nx + 1, pg], tx - 1)
        return pltpu.make_async_remote_copy(
            src, dst, x_send.at[side, off], x_recv.at[side, off],
            device_id=(to, ty, lax.rem(pg + off, pg_n)), device_id_type=MESH)

    def y_copy(side, off):
        src, dst, to = (face_hi, edge_lo.at[pg], ty + 1) if side == 0 else (face_lo, edge_hi.at[pg], ty - 1)
        return pltpu.make_async_remote_copy(
            src, dst, y_send.at[side, off], y_recv.at[side, off],
            device_id=(tx, to, lax.rem(pg + off, pg_n)), device_id_type=MESH)

    sides = ((x_copy, 0, has_xh, has_xl), (x_copy, 1, has_xl, has_xh),
             (y_copy, 0, has_yh, has_yl), (y_copy, 1, has_yl, has_yh))
    for off in range(1, pg_n):
        mode_copy(off).start()
    for copy, side, sends, _ in sides:
        @pl.when(sends)
        def _():
            for off in range(pg_n):
                copy(side, off).start()
    wide[pl.ds(1, nx), pg] = own_ref[...]
    acc[...] = jnp.zeros_like(acc)
    for off in range(1, pg_n):
        mode_copy(off).wait()
    for copy, side, sends, gets in sides:
        @pl.when(sends)
        def _():
            for off in range(pg_n):
                copy(side, off).wait_send()

        @pl.when(gets)
        def _():
            for off in range(pg_n):
                copy(side, off).wait_recv()

    place = lax.rem(lane, CZ)
    chunk_j = 256 // rows_n
    chunks = pg_n * own_n // chunk_j

    def grads(x, xx):
        for p in range(pg_n):
            rows = pl.ds(p * own_n // blk, own_n // blk)
            for c in range(3):
                u = wide[x + 1, p, c].astype(F32)
                us[xx, c, rows] = u.reshape(own_n // blk, blk, lanes)
                gx = wide[x + 2, p, c].astype(F32) - wide[x, p, c].astype(F32)
                e_hi = pltpu.roll(edge_hi[p, c].astype(F32), lanes - CZ - x * CZ, 1)
                e_lo = pltpu.roll(edge_lo[p, c].astype(F32), lax.rem(lanes - x * CZ, lanes), 1)
                up = jnp.where(lane >= lanes - CZ, e_hi, pltpu.roll(u, lanes - CZ, 1))
                down = jnp.where(lane < CZ, e_lo, pltpu.roll(u, CZ, 1))
                gy = up - down
                upper = jnp.where(place == CZ - 1, pltpu.roll(u, CZ - 1, 1), pltpu.roll(u, lanes - 1, 1))
                lower = jnp.where(place == 0, pltpu.roll(u, lanes - CZ + 1, 1), pltpu.roll(u, 1, 1))
                gz = upper - lower
                for d, g in enumerate((gx, gy, gz)):
                    g = (g * 0.5).astype(BF16).astype(F32)
                    gs[xx, d * 3 + c, rows] = g.reshape(own_n // blk, blk, lanes)

    def step(xp, carry):
        for xx in range(2):
            grads(xp * 2 + xx, xx)
            for b in range(per_group):
                s = order_ref[pg * per_group + b]
                for d in range(3):
                    row_us[xx, d, b] = us[xx, d, s]
                for i in range(9):
                    row_gs[xx, i, b] = gs[xx, i, s]

        def one_chunk(ch, carry):
            for xx in range(2):
                row_u = [[row_us[xx, d, b] for b in range(per_group)] for d in range(3)]
                row_g = [[row_gs[xx, i, b] for b in range(per_group)] for i in range(9)]
                for jj in range(chunk_j):
                    jb, jr = ch * (chunk_j // blk) + jj // blk, pl.ds(jj % blk, 1)
                    ju = [jnp.broadcast_to(us[xx, d, jb, jr], (blk, lanes)) for d in range(3)]
                    jg = [jnp.broadcast_to(gs[xx, i, jb, jr], (blk, lanes)) for i in range(9)]
                    for c in range(3):
                        both = []
                        for b in range(per_group):
                            total = row_u[0][b] * jg[c] + ju[0] * row_g[c][b]
                            for d in range(1, 3):
                                total = total + row_u[d][b] * jg[d * 3 + c]
                                total = total + ju[d] * row_g[d * 3 + c][b]
                            both.append(total)
                        pairs[c, pl.ds(jj * rows_n, rows_n), pl.ds(xx * lanes, lanes)] = (
                            jnp.concatenate(both, 0).astype(BF16))
            total = acc[ch]
            for c in range(3):
                basis = jnp.concatenate([adj_ref[c, xp * 2], adj_ref[c, xp * 2 + 1]], 1)
                total = total + lax.dot_general(
                    basis, pairs[c], (((1,), (1,)), ((), ())), preferred_element_type=F32)
            acc[ch] = total
            return carry

        return lax.fori_loop(0, chunks, one_chunk, carry)

    lax.fori_loop(0, nx // 2, step, 0)

    _, _, k_width, width = stage.shape
    for q in range(ty_n):
        first = q * width
        block = acc[first // 256] * weight
        for t in range(tx_n):
            stage[q, t] = block[t * k_width:(t + 1) * k_width, first % 256:first % 256 + width].astype(stage.dtype)

    def part_copy(off):
        to = lax.rem(me + off, group_n)
        to_x, to_y = to // ty_n, lax.rem(to, ty_n)
        return pltpu.make_async_remote_copy(
            stage.at[to_y, to_x], parts.at[me], part_send.at[off], part_recv.at[off],
            device_id=(to_x, to_y, pg), device_id_type=MESH)

    for off in range(1, group_n):
        part_copy(off).start()
    parts[me] = stage[ty, tx]
    for off in range(1, group_n):
        part_copy(off).wait()
    result = parts[0].astype(F32)
    for source in range(1, group_n):
        result = result + parts[source].astype(F32)
    out_ref[...] = result


def shards(direct_modes, adjoint_modes, block_order):
    tx_n, ty_n, pg_n = lax.axis_size("tx"), lax.axis_size("ty"), lax.axis_size("pg")
    own_n, _, nx, lanes = direct_modes.shape
    adj_n = adjoint_modes.shape[0]
    mode_n = own_n * pg_n
    weight = 1.0 / math.sqrt(3.0 * nx * tx_n * lanes * ty_n)
    j_width, k_width = mode_n // ty_n, adj_n // tx_n
    width = j_width * own_n
    blk = mode_n // NBLK
    own = jnp.transpose(direct_modes, (2, 1, 0, 3))
    adj = jnp.transpose(adjoint_modes, (1, 2, 0, 3))
    vmem = pl.BlockSpec(memory_space=pltpu.VMEM)
    dma = pltpu.SemaphoreType.DMA
    summed = pl.pallas_call(
        functools.partial(kernel, tx_n, ty_n, pg_n, weight),
        out_shape=jax.ShapeDtypeStruct((k_width, width), F32),
        in_specs=[pl.BlockSpec(memory_space=pltpu.SMEM), vmem, vmem],
        out_specs=vmem,
        scratch_shapes=[
            pltpu.VMEM((nx + 2, pg_n, 3, own_n, lanes), BF16),
            pltpu.VMEM((3, own_n, lanes), BF16),
            pltpu.VMEM((3, own_n, lanes), BF16),
            pltpu.VMEM((pg_n, 3, own_n, lanes), BF16),
            pltpu.VMEM((pg_n, 3, own_n, lanes), BF16),
            pltpu.VMEM((2, 3, NBLK, blk, lanes), F32),
            pltpu.VMEM((2, 9, NBLK, blk, lanes), F32),
            pltpu.VMEM((2, 3, NBLK // pg_n, blk, lanes), F32),
            pltpu.VMEM((2, 9, NBLK // pg_n, blk, lanes), F32),
            pltpu.VMEM((3, 256, 2 * lanes), BF16),
            pltpu.VMEM((mode_n * own_n // 256, adj_n, 256), F32),
            pltpu.VMEM((ty_n, tx_n, k_width, width), BF16),
            pltpu.VMEM((tx_n * ty_n, k_width, width), BF16),
            dma((pg_n,)), dma((pg_n,)),
            dma((2, pg_n)), dma((2, pg_n)),
            dma((2, pg_n)), dma((2, pg_n)),
            dma((tx_n * ty_n,)), dma((tx_n * ty_n,)),
        ],
        compiler_params=pltpu.CompilerParams(
            collective_id=0, has_side_effects=True, vmem_limit_bytes=40 * 2**20),
    )(block_order, own, adj)
    return jnp.transpose(summed.reshape(k_width, j_width, own_n), (2, 1, 0))


def solution(mesh):
    placed = (P("pg", None, "tx", "ty"), P(None, None, "tx", "ty"), P())
    return jax.shard_map(
        shards, mesh=mesh, in_specs=placed, out_specs=P("pg", "ty", "tx"), check_vma=False
    )
```

```python
import functools
import math

import jax
import jax.numpy as jnp
from jax import lax
from jax.experimental import pallas as pl
from jax.experimental.pallas import tpu as pltpu
from jax.sharding import PartitionSpec as P

NBLK = 8
CZ = 4
QUARTERS = 4
MESH = pl.DeviceIdType.MESH
F32 = jnp.float32
BF16 = jnp.bfloat16


def kernel(
    tx_n, ty_n, pg_n, weight,
    order_ref, own_ref, adj_ref, out_ref,
    wide, face_lo, face_hi, edge_lo, edge_hi, us, gs, row_us, row_gs, pairs_a, pairs_b, acc, stage, parts,
    mode_send, mode_recv, x_send, x_recv, y_send, y_recv, part_send, part_recv,
):
    tx, ty, pg = lax.axis_index("tx"), lax.axis_index("ty"), lax.axis_index("pg")
    nx, _, own_n, lanes = own_ref.shape
    group_n = tx_n * ty_n
    me = tx * ty_n + ty
    rows_n = own_n
    quarter = nx // QUARTERS
    blk = pg_n * own_n // NBLK
    per_group = NBLK // pg_n

    has_xl, has_xh = tx > 0, tx < tx_n - 1
    has_yl, has_yh = ty > 0, ty < ty_n - 1

    barrier = pltpu.get_barrier_semaphore()
    for off in range(1, pg_n):
        pl.semaphore_signal(barrier, inc=1, device_id=(tx, ty, lax.rem(pg + off, pg_n)), device_id_type=MESH)
    for off in range(1, group_n):
        to = lax.rem(me + off, group_n)
        pl.semaphore_signal(barrier, inc=1, device_id=(to // ty_n, lax.rem(to, ty_n), pg), device_id_type=MESH)
    for has, dx, dy in ((has_xl, -1, 0), (has_xh, 1, 0), (has_yl, 0, -1), (has_yh, 0, 1)):
        @pl.when(has)
        def _():
            for off in range(1, pg_n):
                pl.semaphore_signal(
                    barrier, inc=1, device_id=(tx + dx, ty + dy, lax.rem(pg + off, pg_n)), device_id_type=MESH)

    lane = lax.broadcasted_iota(jnp.int32, (own_n, lanes), 1)
    for c in range(3):
        low = jnp.zeros((own_n, lanes), F32)
        high = jnp.zeros((own_n, lanes), F32)
        for x in range(nx):
            tile = own_ref[x, c].astype(F32)
            here = (lane >= x * CZ) & (lane < (x + 1) * CZ)
            low = jnp.where(here, pltpu.roll(tile, (x * CZ) % lanes, 1) if x else tile, low)
            high = jnp.where(here, pltpu.roll(tile, (x * CZ + CZ) % lanes, 1), high)
        face_lo[c] = low.astype(BF16)
        face_hi[c] = high.astype(BF16)

    zero = jnp.zeros((pg_n, 3, own_n, lanes), BF16)

    @pl.when(jnp.logical_not(has_xl))
    def _():
        wide[0] = zero

    @pl.when(jnp.logical_not(has_xh))
    def _():
        wide[nx + 1] = zero

    @pl.when(jnp.logical_not(has_yl))
    def _():
        edge_lo[...] = zero

    @pl.when(jnp.logical_not(has_yh))
    def _():
        edge_hi[...] = zero

    neighbours = 1 * (has_xl.astype(jnp.int32) + has_xh.astype(jnp.int32)
                      + has_yl.astype(jnp.int32) + has_yh.astype(jnp.int32))
    pl.semaphore_wait(barrier, (pg_n - 1) + (group_n - 1) + neighbours * (pg_n - 1))

    def mode_copy(off, q):
        return pltpu.make_async_remote_copy(
            own_ref.at[pl.ds(q * quarter, quarter)], wide.at[pl.ds(1 + q * quarter, quarter), pg],
            mode_send.at[off, q], mode_recv.at[off, q],
            device_id=(tx, ty, lax.rem(pg + off, pg_n)), device_id_type=MESH)

    def x_copy(side, off):
        src, dst, to = (own_ref.at[nx - 1], wide.at[0, pg], tx + 1) if side == 0 else (
            own_ref.at[0], wide.at[nx + 1, pg], tx - 1)
        return pltpu.make_async_remote_copy(
            src, dst, x_send.at[side, off], x_recv.at[side, off],
            device_id=(to, ty, lax.rem(pg + off, pg_n)), device_id_type=MESH)

    def y_copy(side, off):
        src, dst, to = (face_hi, edge_lo.at[pg], ty + 1) if side == 0 else (face_lo, edge_hi.at[pg], ty - 1)
        return pltpu.make_async_remote_copy(
            src, dst, y_send.at[side, off], y_recv.at[side, off],
            device_id=(tx, to, lax.rem(pg + off, pg_n)), device_id_type=MESH)

    sides = ((x_copy, 0, has_xh, has_xl), (x_copy, 1, has_xl, has_xh),
             (y_copy, 0, has_yh, has_yl), (y_copy, 1, has_yl, has_yh))
    for copy, side, sends, _ in sides:
        @pl.when(sends)
        def _():
            for off in range(pg_n):
                copy(side, off).start()
    for q in range(QUARTERS):
        for off in range(1, pg_n):
            mode_copy(off, q).start()
    wide[pl.ds(1, nx), pg] = own_ref[...]
    pairs_b[...] = jnp.zeros_like(pairs_b)

    def arrived(sides):
        for copy, side, _, gets in sides:
            @pl.when(gets)
            def _():
                for off in range(pg_n):
                    copy(side, off).wait_recv()

    arrived((sides[0], sides[2], sides[3]))
    for off in range(1, pg_n):
        mode_copy(off, 0).wait_recv()

    place = lax.rem(lane, CZ)
    chunk_j = 256 // rows_n
    chunks = pg_n * own_n // chunk_j
    per_chunk = ty_n // chunks
    _, _, k_width, width = stage.shape

    def grads(x, carry):
        for p in range(pg_n):
            rows = pl.ds(p * own_n // blk, own_n // blk)
            for c in range(3):
                u = wide[x + 1, p, c].astype(F32)
                us[x, c, rows] = u.reshape(own_n // blk, blk, lanes)
                gx = wide[x + 2, p, c].astype(F32) - wide[x, p, c].astype(F32)
                e_hi = pltpu.roll(edge_hi[p, c].astype(F32), lanes - CZ - x * CZ, 1)
                e_lo = pltpu.roll(edge_lo[p, c].astype(F32), lax.rem(lanes - x * CZ, lanes), 1)
                up = jnp.where(lane >= lanes - CZ, e_hi, pltpu.roll(u, lanes - CZ, 1))
                down = jnp.where(lane < CZ, e_lo, pltpu.roll(u, CZ, 1))
                gy = up - down
                upper = jnp.where(place == CZ - 1, pltpu.roll(u, CZ - 1, 1), pltpu.roll(u, lanes - 1, 1))
                lower = jnp.where(place == 0, pltpu.roll(u, lanes - CZ + 1, 1), pltpu.roll(u, 1, 1))
                gz = upper - lower
                for d, g in enumerate((gx, gy, gz)):
                    g = (g * 0.5).astype(BF16).astype(F32)
                    gs[x, d * 3 + c, rows] = g.reshape(own_n // blk, blk, lanes)
        for b in range(per_group):
            s = order_ref[pg * per_group + b]
            for d in range(3):
                row_us[x, d, b] = us[x, d, s]
            for i in range(9):
                row_gs[x, i, b] = gs[x, i, s]
        return carry

    def form(pairs, x0, ch):
        for xx in range(2):
            x = x0 + xx
            row_u = [[row_us[x, d, b] for b in range(per_group)] for d in range(3)]
            row_g = [[row_gs[x, i, b] for b in range(per_group)] for i in range(9)]
            for jj in range(chunk_j):
                jb, jr = ch * (chunk_j // blk) + jj // blk, pl.ds(jj % blk, 1)
                ju = [jnp.broadcast_to(us[x, d, jb, jr], (blk, lanes)) for d in range(3)]
                jg = [jnp.broadcast_to(gs[x, i, jb, jr], (blk, lanes)) for i in range(9)]
                for c in range(3):
                    both = []
                    for b in range(per_group):
                        total = row_u[0][b] * jg[c] + ju[0] * row_g[c][b]
                        for d in range(1, 3):
                            total = total + row_u[d][b] * jg[d * 3 + c]
                            total = total + ju[d] * row_g[d * 3 + c][b]
                        both.append(total)
                    pairs[pl.ds(jj * rows_n, rows_n), pl.ds((2 * c + xx) * lanes, lanes)] = (
                        jnp.concatenate(both, 0).astype(BF16))

    def projected(pairs, x0):
        basis = jnp.concatenate([adj_ref[c, x0 + xx] for c in range(3) for xx in range(2)], 1)
        return lax.dot_general(
            basis, pairs[...], (((1,), (1,)), ((), ())), preferred_element_type=F32)

    def part_copy(off):
        to = lax.rem(me + off, group_n)
        to_x, to_y = to // ty_n, lax.rem(to, ty_n)
        return pltpu.make_async_remote_copy(
            stage.at[to_y, to_x], parts.at[me], part_send.at[off], part_recv.at[off],
            device_id=(to_x, to_y, pg), device_id_type=MESH)

    def step(index, carry):
        turn, q = index // QUARTERS, lax.rem(index, QUARTERS)
        ch = lax.rem(ty // per_chunk + 1 + turn, chunks)

        @pl.when(turn == 0)
        def _():
            @pl.when(q < QUARTERS - 1)
            def _():
                for off in range(1, pg_n):
                    mode_copy(off, q + 1).wait_recv()

            @pl.when(q == QUARTERS - 1)
            def _():
                arrived((sides[1],))

            lax.fori_loop(q * quarter, (q + 1) * quarter, grads, 0)

        def two(i, carry):
            x0 = q * quarter + 4 * i
            form(pairs_a, x0, ch)
            before = acc[...] + projected(pairs_b, lax.rem(x0 + nx - 2, nx))
            acc[...] = jnp.where(x0 == 0, 0.0, before)
            form(pairs_b, x0 + 2, ch)
            acc[...] += projected(pairs_a, x0)
            return carry

        if quarter == 4:
            two(0, 0)
        else:
            lax.fori_loop(0, quarter // 4, two, 0)

        @pl.when(q == QUARTERS - 1)
        def _():
            block = (acc[...] + projected(pairs_b, nx - 2)) * weight
            for i in range(per_chunk):
                to_y = ch * per_chunk + i
                for t in range(tx_n):
                    stage[to_y, t] = block[
                        t * k_width:(t + 1) * k_width, i * width:(i + 1) * width].astype(stage.dtype)
                    to = t * ty_n + to_y

                    @pl.when(to != me)
                    def _():
                        part_copy(lax.rem(to - me + group_n, group_n)).start()
        return carry

    lax.fori_loop(0, chunks * QUARTERS, step, 0)
    parts[me] = stage[ty, tx]

    for q in range(QUARTERS):
        for off in range(1, pg_n):
            mode_copy(off, q).wait_send()
    for copy, side, sends, _ in sides:
        @pl.when(sends)
        def _():
            for off in range(pg_n):
                copy(side, off).wait_send()
    for off in range(1, group_n):
        part_copy(off).wait()
    result = parts[0].astype(F32)
    for source in range(1, group_n):
        result = result + parts[source].astype(F32)
    out_ref[...] = result


def shards(direct_modes, adjoint_modes, block_order):
    tx_n, ty_n, pg_n = lax.axis_size("tx"), lax.axis_size("ty"), lax.axis_size("pg")
    own_n, _, nx, lanes = direct_modes.shape
    adj_n = adjoint_modes.shape[0]
    mode_n = own_n * pg_n
    weight = 1.0 / math.sqrt(3.0 * nx * tx_n * lanes * ty_n)
    j_width, k_width = mode_n // ty_n, adj_n // tx_n
    width = j_width * own_n
    blk = mode_n // NBLK
    own = jnp.transpose(direct_modes, (2, 1, 0, 3))
    adj = jnp.transpose(adjoint_modes, (1, 2, 0, 3))
    vmem = pl.BlockSpec(memory_space=pltpu.VMEM)
    dma = pltpu.SemaphoreType.DMA
    summed = pl.pallas_call(
        functools.partial(kernel, tx_n, ty_n, pg_n, weight),
        out_shape=jax.ShapeDtypeStruct((k_width, width), F32),
        in_specs=[pl.BlockSpec(memory_space=pltpu.SMEM), vmem, vmem],
        out_specs=vmem,
        scratch_shapes=[
            pltpu.VMEM((nx + 2, pg_n, 3, own_n, lanes), BF16),
            pltpu.VMEM((3, own_n, lanes), BF16),
            pltpu.VMEM((3, own_n, lanes), BF16),
            pltpu.VMEM((pg_n, 3, own_n, lanes), BF16),
            pltpu.VMEM((pg_n, 3, own_n, lanes), BF16),
            pltpu.VMEM((nx, 3, NBLK, blk, lanes), F32),
            pltpu.VMEM((nx, 9, NBLK, blk, lanes), F32),
            pltpu.VMEM((nx, 3, NBLK // pg_n, blk, lanes), F32),
            pltpu.VMEM((nx, 9, NBLK // pg_n, blk, lanes), F32),
            pltpu.VMEM((256, 6 * lanes), BF16),
            pltpu.VMEM((256, 6 * lanes), BF16),
            pltpu.VMEM((adj_n, 256), F32),
            pltpu.VMEM((ty_n, tx_n, k_width, width), BF16),
            pltpu.VMEM((tx_n * ty_n, k_width, width), BF16),
            dma((pg_n, QUARTERS)), dma((pg_n, QUARTERS)),
            dma((2, pg_n)), dma((2, pg_n)),
            dma((2, pg_n)), dma((2, pg_n)),
            dma((tx_n * ty_n,)), dma((tx_n * ty_n,)),
        ],
        compiler_params=pltpu.CompilerParams(
            collective_id=0, has_side_effects=True, vmem_limit_bytes=40 * 2**20),
    )(block_order, own, adj)
    return jnp.transpose(summed.reshape(k_width, j_width, own_n), (2, 1, 0))


def solution(mesh):
    placed = (P("pg", None, "tx", "ty"), P(None, None, "tx", "ty"), P())
    return jax.shard_map(
        shards, mesh=mesh, in_specs=placed, out_specs=P("pg", "ty", "tx"), check_vma=False
    )
```

```python
import functools
import math

import jax
import jax.numpy as jnp
from jax import lax
from jax.experimental import pallas as pl
from jax.experimental.pallas import tpu as pltpu
from jax.sharding import PartitionSpec as P

NBLK = 8
CZ = 4
QUARTERS = 4
CHUNK = 512
PIECES = 1
MESH = pl.DeviceIdType.MESH
F32 = jnp.float32
BF16 = jnp.bfloat16


def kernel(
    tx_n, ty_n, pg_n, weight,
    order_ref, own_any, adj_in, out_ref,
    own_in, own_sem, own_flat, own_ref, adj_raw, adj_flat, adj_sem, wide, face_lo, face_hi, edge_lo, edge_hi, us, gs, row_us, row_gs, pairs_a, pairs_b, acc, stage, parts,
    mode_send, mode_recv, x_send, x_recv, y_send, y_recv, part_send, part_recv,
):
    tx, ty, pg = lax.axis_index("tx"), lax.axis_index("ty"), lax.axis_index("pg")
    nx, _, own_n, lanes = own_ref.shape
    adj_n = adj_raw.shape[0]
    own_copy = pltpu.make_async_copy(own_any, own_in, own_sem)
    own_copy.start()
    adj_copy = pltpu.make_async_copy(adj_in, adj_raw, adj_sem)
    adj_copy.start()
    group_n = tx_n * ty_n
    me = tx * ty_n + ty
    rows_n = own_n
    quarter = nx // QUARTERS
    blk = pg_n * own_n // NBLK
    per_group = NBLK // pg_n

    has_xl, has_xh = tx > 0, tx < tx_n - 1
    has_yl, has_yh = ty > 0, ty < ty_n - 1

    barrier = pltpu.get_barrier_semaphore()
    for off in range(1, pg_n):
        pl.semaphore_signal(barrier, inc=1, device_id=(tx, ty, lax.rem(pg + off, pg_n)), device_id_type=MESH)
    for off in range(1, group_n):
        to = lax.rem(me + off, group_n)
        pl.semaphore_signal(barrier, inc=1, device_id=(to // ty_n, lax.rem(to, ty_n), pg), device_id_type=MESH)
    for has, dx, dy in ((has_xl, -1, 0), (has_xh, 1, 0), (has_yl, 0, -1), (has_yh, 0, 1)):
        @pl.when(has)
        def _():
            for off in range(1, pg_n):
                pl.semaphore_signal(
                    barrier, inc=1, device_id=(tx + dx, ty + dy, lax.rem(pg + off, pg_n)), device_id_type=MESH)

    own_copy.wait()
    for m in range(own_n):
        for c in range(3):
            own_flat[pl.ds(c * own_n + m, nx, stride=3 * own_n), :] = own_in[m, c].astype(F32)
    for x in range(nx):
        for c in range(3):
            own_ref[x, c] = own_flat[pl.ds((x * 3 + c) * own_n, own_n), :].astype(BF16)

    lane = lax.broadcasted_iota(jnp.int32, (own_n, lanes), 1)
    for c in range(3):
        low = jnp.zeros((own_n, lanes), F32)
        high = jnp.zeros((own_n, lanes), F32)
        for x in range(nx):
            tile = own_ref[x, c].astype(F32)
            here = (lane >= x * CZ) & (lane < (x + 1) * CZ)
            low = jnp.where(here, pltpu.roll(tile, (x * CZ) % lanes, 1) if x else tile, low)
            high = jnp.where(here, pltpu.roll(tile, (x * CZ + CZ) % lanes, 1), high)
        face_lo[c] = low.astype(BF16)
        face_hi[c] = high.astype(BF16)

    zero = jnp.zeros((pg_n, 3, own_n, lanes), BF16)

    @pl.when(jnp.logical_not(has_xl))
    def _():
        wide[0] = zero

    @pl.when(jnp.logical_not(has_xh))
    def _():
        wide[nx + 1] = zero

    @pl.when(jnp.logical_not(has_yl))
    def _():
        edge_lo[...] = zero

    @pl.when(jnp.logical_not(has_yh))
    def _():
        edge_hi[...] = zero

    neighbours = 1 * (has_xl.astype(jnp.int32) + has_xh.astype(jnp.int32)
                      + has_yl.astype(jnp.int32) + has_yh.astype(jnp.int32))
    pl.semaphore_wait(barrier, (pg_n - 1) + (group_n - 1) + neighbours * (pg_n - 1))

    def mode_copy(off, q):
        return pltpu.make_async_remote_copy(
            own_ref.at[pl.ds(q * quarter, quarter)], wide.at[pl.ds(1 + q * quarter, quarter), pg],
            mode_send.at[off, q], mode_recv.at[off, q],
            device_id=(tx, ty, lax.rem(pg + off, pg_n)), device_id_type=MESH)

    def x_copy(side, off):
        src, dst, to = (own_ref.at[nx - 1], wide.at[0, pg], tx + 1) if side == 0 else (
            own_ref.at[0], wide.at[nx + 1, pg], tx - 1)
        return pltpu.make_async_remote_copy(
            src, dst, x_send.at[side, off], x_recv.at[side, off],
            device_id=(to, ty, lax.rem(pg + off, pg_n)), device_id_type=MESH)

    def y_copy(side, off):
        src, dst, to = (face_hi, edge_lo.at[pg], ty + 1) if side == 0 else (face_lo, edge_hi.at[pg], ty - 1)
        return pltpu.make_async_remote_copy(
            src, dst, y_send.at[side, off], y_recv.at[side, off],
            device_id=(tx, to, lax.rem(pg + off, pg_n)), device_id_type=MESH)

    sides = ((x_copy, 0, has_xh, has_xl), (x_copy, 1, has_xl, has_xh),
             (y_copy, 0, has_yh, has_yl), (y_copy, 1, has_yl, has_yh))
    for copy, side, sends, _ in sides:
        @pl.when(sends)
        def _():
            for off in range(pg_n):
                copy(side, off).start()
    for q in range(QUARTERS):
        for off in range(1, pg_n):
            mode_copy(off, q).start()
    wide[pl.ds(1, nx), pg] = own_ref[...]
    pairs_b[...] = jnp.zeros_like(pairs_b)
    adj_copy.wait()

    def turn_basis(i, carry):
        for more in range(4):
            k = i * 4 + more
            for c in range(3):
                adj_flat[pl.ds(c * nx * adj_n + k, nx, stride=adj_n), :] = adj_raw[k, c].astype(F32)
        return carry

    lax.fori_loop(0, adj_n // 4, turn_basis, 0)

    def arrived(sides):
        for copy, side, _, gets in sides:
            @pl.when(gets)
            def _():
                for off in range(pg_n):
                    copy(side, off).wait_recv()

    arrived((sides[0], sides[2], sides[3]))
    for off in range(1, pg_n):
        mode_copy(off, 0).wait_recv()

    place = lax.rem(lane, CZ)
    chunk_j = CHUNK // rows_n
    chunks = pg_n * own_n // chunk_j
    per_chunk = ty_n // chunks
    _, _, k_width, width = stage.shape

    def grads(x, carry):
        for p in range(pg_n):
            rows = pl.ds(p * own_n // blk, own_n // blk)
            for c in range(3):
                u = wide[x + 1, p, c].astype(F32)
                us[x, c, rows] = u.reshape(own_n // blk, blk, lanes)
                gx = wide[x + 2, p, c].astype(F32) - wide[x, p, c].astype(F32)
                e_hi = pltpu.roll(edge_hi[p, c].astype(F32), lanes - CZ - x * CZ, 1)
                e_lo = pltpu.roll(edge_lo[p, c].astype(F32), lax.rem(lanes - x * CZ, lanes), 1)
                up = jnp.where(lane >= lanes - CZ, e_hi, pltpu.roll(u, lanes - CZ, 1))
                down = jnp.where(lane < CZ, e_lo, pltpu.roll(u, CZ, 1))
                gy = up - down
                upper = jnp.where(place == CZ - 1, pltpu.roll(u, CZ - 1, 1), pltpu.roll(u, lanes - 1, 1))
                lower = jnp.where(place == 0, pltpu.roll(u, lanes - CZ + 1, 1), pltpu.roll(u, 1, 1))
                gz = upper - lower
                for d, g in enumerate((gx, gy, gz)):
                    g = (g * 0.5).astype(BF16).astype(F32)
                    gs[x, d * 3 + c, rows] = g.reshape(own_n // blk, blk, lanes)
        for b in range(per_group):
            s = order_ref[pg * per_group + b]
            for d in range(3):
                row_us[x, d, b] = us[x, d, s]
            for i in range(9):
                row_gs[x, i, b] = gs[x, i, s]
        return carry

    def projected(pairs, x0, piece=None):
        parts_of = 6 // PIECES
        ks = range(6) if piece is None else range(piece * parts_of, (piece + 1) * parts_of)
        basis = jnp.concatenate(
            [adj_flat[pl.ds(pl.multiple_of((k // 2 * nx + x0 + k % 2) * adj_n, adj_n), adj_n), :]
             for k in ks], 1).astype(BF16)
        return lax.dot_general(
            basis, pairs[:, ks[0] * lanes:(ks[-1] + 1) * lanes], (((1,), (1,)), ((), ())),
            preferred_element_type=F32)

    def form(pairs, x0, ch, other, y0):
        made = jnp.zeros((adj_n, CHUNK), F32)
        for xx in range(2):
            x = x0 + xx
            row_u = [[row_us[x, d, b] for b in range(per_group)] for d in range(3)]
            row_g = [[row_gs[x, i, b] for b in range(per_group)] for i in range(9)]
            for jj in range(chunk_j):
                at = xx * chunk_j + jj
                for piece in range(PIECES):
                    if at == piece * 2 * chunk_j // PIECES:
                        made = made + projected(other, y0, piece)
                jb, jr = ch * (chunk_j // blk) + jj // blk, pl.ds(jj % blk, 1)
                ju = [jnp.broadcast_to(us[x, d, jb, jr], (blk, lanes)) for d in range(3)]
                jg = [jnp.broadcast_to(gs[x, i, jb, jr], (blk, lanes)) for i in range(9)]
                for c in range(3):
                    both = []
                    for b in range(per_group):
                        total = row_u[0][b] * jg[c] + ju[0] * row_g[c][b]
                        for d in range(1, 3):
                            total = total + row_u[d][b] * jg[d * 3 + c]
                            total = total + ju[d] * row_g[d * 3 + c][b]
                        both.append(total)
                    pairs[pl.ds(jj * rows_n, rows_n), pl.ds((2 * c + xx) * lanes, lanes)] = (
                        jnp.concatenate(both, 0).astype(BF16))
        return made

    def part_copy(off):
        to = lax.rem(me + off, group_n)
        to_x, to_y = to // ty_n, lax.rem(to, ty_n)
        return pltpu.make_async_remote_copy(
            stage.at[to_y, to_x], parts.at[me], part_send.at[off], part_recv.at[off],
            device_id=(to_x, to_y, pg), device_id_type=MESH)

    def step(index, carry):
        turn, q = index // QUARTERS, lax.rem(index, QUARTERS)
        ch = lax.rem(ty // per_chunk + 1 + turn, chunks)

        @pl.when(turn == 0)
        def _():
            @pl.when(q < QUARTERS - 1)
            def _():
                for off in range(1, pg_n):
                    mode_copy(off, q + 1).wait_recv()

            @pl.when(q == QUARTERS - 1)
            def _():
                arrived((sides[1],))

            lax.fori_loop(q * quarter, (q + 1) * quarter, grads, 0)

        def two(i, carry):
            x0 = q * quarter + 4 * i
            last = form(pairs_a, x0, ch, pairs_b, lax.rem(x0 + nx - 2, nx))
            acc[...] = jnp.where(x0 == 0, 0.0, acc[...] + last)
            acc[...] += form(pairs_b, x0 + 2, ch, pairs_a, x0)
            return carry

        if quarter == 4:
            two(0, 0)
        else:
            lax.fori_loop(0, quarter // 4, two, 0)

        @pl.when(q == QUARTERS - 1)
        def _():
            block = (acc[...] + projected(pairs_b, nx - 2)) * weight
            for i in range(per_chunk):
                to_y = ch * per_chunk + i
                for t in range(tx_n):
                    stage[to_y, t] = block[
                        t * k_width:(t + 1) * k_width, i * width:(i + 1) * width].astype(stage.dtype)
                    to = t * ty_n + to_y

                    @pl.when(to != me)
                    def _():
                        part_copy(lax.rem(to - me + group_n, group_n)).start()
        return carry

    lax.fori_loop(0, chunks * QUARTERS, step, 0)
    parts[me] = stage[ty, tx]

    for q in range(QUARTERS):
        for off in range(1, pg_n):
            mode_copy(off, q).wait_send()
    for copy, side, sends, _ in sides:
        @pl.when(sends)
        def _():
            for off in range(pg_n):
                copy(side, off).wait_send()
    for off in range(1, group_n):
        part_copy(off).wait()
    result = parts[0].astype(F32)
    for source in range(1, group_n):
        result = result + parts[source].astype(F32)
    out_ref[...] = result


def shards(direct_modes, adjoint_modes, block_order):
    tx_n, ty_n, pg_n = lax.axis_size("tx"), lax.axis_size("ty"), lax.axis_size("pg")
    own_n, _, nx, lanes = direct_modes.shape
    adj_n = adjoint_modes.shape[0]
    mode_n = own_n * pg_n
    weight = 1.0 / math.sqrt(3.0 * nx * tx_n * lanes * ty_n)
    j_width, k_width = mode_n // ty_n, adj_n // tx_n
    width = j_width * own_n
    blk = mode_n // NBLK
    vmem = pl.BlockSpec(memory_space=pltpu.VMEM)
    dma = pltpu.SemaphoreType.DMA
    summed = pl.pallas_call(
        functools.partial(kernel, tx_n, ty_n, pg_n, weight),
        out_shape=jax.ShapeDtypeStruct((k_width, width), F32),
        in_specs=[pl.BlockSpec(memory_space=pltpu.SMEM)] + [pl.BlockSpec(memory_space=pl.ANY)] * 2,
        out_specs=vmem,
        scratch_shapes=[
            pltpu.VMEM((own_n, 3, nx, lanes), BF16),
            dma,
            pltpu.VMEM((nx * 3 * own_n, lanes), F32),
            pltpu.VMEM((nx, 3, own_n, lanes), BF16),
            pltpu.VMEM((adj_n, 3, nx, lanes), BF16),
            pltpu.VMEM((3 * nx * adj_n, lanes), F32),
            dma,
            pltpu.VMEM((nx + 2, pg_n, 3, own_n, lanes), BF16),
            pltpu.VMEM((3, own_n, lanes), BF16),
            pltpu.VMEM((3, own_n, lanes), BF16),
            pltpu.VMEM((pg_n, 3, own_n, lanes), BF16),
            pltpu.VMEM((pg_n, 3, own_n, lanes), BF16),
            pltpu.VMEM((nx, 3, NBLK, blk, lanes), F32),
            pltpu.VMEM((nx, 9, NBLK, blk, lanes), F32),
            pltpu.VMEM((nx, 3, NBLK // pg_n, blk, lanes), F32),
            pltpu.VMEM((nx, 9, NBLK // pg_n, blk, lanes), F32),
            pltpu.VMEM((CHUNK, 6 * lanes), BF16),
            pltpu.VMEM((CHUNK, 6 * lanes), BF16),
            pltpu.VMEM((adj_n, CHUNK), F32),
            pltpu.VMEM((ty_n, tx_n, k_width, width), BF16),
            pltpu.VMEM((tx_n * ty_n, k_width, width), BF16),
            dma((pg_n, QUARTERS)), dma((pg_n, QUARTERS)),
            dma((2, pg_n)), dma((2, pg_n)),
            dma((2, pg_n)), dma((2, pg_n)),
            dma((tx_n * ty_n,)), dma((tx_n * ty_n,)),
        ],
        compiler_params=pltpu.CompilerParams(
            collective_id=0, has_side_effects=True, vmem_limit_bytes=60 * 2**20),
    )(block_order, direct_modes, adjoint_modes)
    return jnp.transpose(summed.reshape(k_width, j_width, own_n), (2, 1, 0))


def solution(mesh):
    placed = (P("pg", None, "tx", "ty"), P(None, None, "tx", "ty"), P())
    return jax.shard_map(
        shards, mesh=mesh, in_specs=placed, out_specs=P("pg", "ty", "tx"), check_vma=False
    )
```

```python
import functools
import math

import jax
import jax.numpy as jnp
from jax import lax
from jax.experimental import pallas as pl
from jax.experimental.pallas import tpu as pltpu
from jax.sharding import PartitionSpec as P

NBLK = 8
CZ = 4
QUARTERS = 4
CHUNK = 512
PIECES = 1
MESH = pl.DeviceIdType.MESH
F32 = jnp.float32
BF16 = jnp.bfloat16


def kernel(
    tx_n, ty_n, pg_n, weight,
    order_ref, own_any, adj_in, out_ref,
    own_in, own_sem, own_flat, own_ref, adj_raw, adj_flat, adj_sem, wide, face_lo, face_hi, edge_lo, edge_hi, us, gs, row_us, row_gs, pairs_a, pairs_b, acc, stage, parts,
    mode_send, mode_recv, x_send, x_recv, y_send, y_recv, part_send, part_recv,
):
    tx, ty, pg = lax.axis_index("tx"), lax.axis_index("ty"), lax.axis_index("pg")
    nx, _, own_n, lanes = own_ref.shape
    adj_n = adj_raw.shape[0]
    own_copy = pltpu.make_async_copy(own_any, own_in, own_sem)
    own_copy.start()
    adj_copy = pltpu.make_async_copy(adj_in, adj_raw, adj_sem)
    adj_copy.start()
    group_n = tx_n * ty_n
    me = tx * ty_n + ty
    rows_n = own_n
    quarter = nx // QUARTERS
    blk = pg_n * own_n // NBLK
    per_group = NBLK // pg_n

    has_xl, has_xh = tx > 0, tx < tx_n - 1
    has_yl, has_yh = ty > 0, ty < ty_n - 1

    barrier = pltpu.get_barrier_semaphore()
    for off in range(1, pg_n):
        pl.semaphore_signal(barrier, inc=1, device_id=(tx, ty, lax.rem(pg + off, pg_n)), device_id_type=MESH)
    for off in range(1, group_n):
        to = lax.rem(me + off, group_n)
        pl.semaphore_signal(barrier, inc=1, device_id=(to // ty_n, lax.rem(to, ty_n), pg), device_id_type=MESH)
    for has, dx, dy in ((has_xl, -1, 0), (has_xh, 1, 0), (has_yl, 0, -1), (has_yh, 0, 1)):
        @pl.when(has)
        def _():
            for off in range(1, pg_n):
                pl.semaphore_signal(
                    barrier, inc=1, device_id=(tx + dx, ty + dy, lax.rem(pg + off, pg_n)), device_id_type=MESH)

    own_copy.wait()
    for m in range(own_n):
        for c in range(3):
            own_flat[pl.ds(c * own_n + m, nx, stride=3 * own_n), :] = own_in[m, c].astype(F32)
    for x in range(nx):
        for c in range(3):
            own_ref[x, c] = own_flat[pl.ds((x * 3 + c) * own_n, own_n), :].astype(BF16)

    lane = lax.broadcasted_iota(jnp.int32, (own_n, lanes), 1)
    for c in range(3):
        low = jnp.zeros((own_n, lanes), F32)
        high = jnp.zeros((own_n, lanes), F32)
        for x in range(nx):
            tile = own_ref[x, c].astype(F32)
            here = (lane >= x * CZ) & (lane < (x + 1) * CZ)
            low = jnp.where(here, pltpu.roll(tile, (x * CZ) % lanes, 1) if x else tile, low)
            high = jnp.where(here, pltpu.roll(tile, (x * CZ + CZ) % lanes, 1), high)
        face_lo[c] = low.astype(BF16)
        face_hi[c] = high.astype(BF16)

    zero = jnp.zeros((pg_n, 3, own_n, lanes), BF16)

    @pl.when(jnp.logical_not(has_xl))
    def _():
        wide[0] = zero

    @pl.when(jnp.logical_not(has_xh))
    def _():
        wide[nx + 1] = zero

    @pl.when(jnp.logical_not(has_yl))
    def _():
        edge_lo[...] = zero

    @pl.when(jnp.logical_not(has_yh))
    def _():
        edge_hi[...] = zero

    neighbours = 1 * (has_xl.astype(jnp.int32) + has_xh.astype(jnp.int32)
                      + has_yl.astype(jnp.int32) + has_yh.astype(jnp.int32))
    pl.semaphore_wait(barrier, (pg_n - 1) + (group_n - 1) + neighbours * (pg_n - 1))

    def mode_copy(off, q):
        return pltpu.make_async_remote_copy(
            own_ref.at[pl.ds(q * quarter, quarter)], wide.at[pl.ds(1 + q * quarter, quarter), pg],
            mode_send.at[off, q], mode_recv.at[off, q],
            device_id=(tx, ty, lax.rem(pg + off, pg_n)), device_id_type=MESH)

    def x_copy(side, off):
        src, dst, to = (own_ref.at[nx - 1], wide.at[0, pg], tx + 1) if side == 0 else (
            own_ref.at[0], wide.at[nx + 1, pg], tx - 1)
        return pltpu.make_async_remote_copy(
            src, dst, x_send.at[side, off], x_recv.at[side, off],
            device_id=(to, ty, lax.rem(pg + off, pg_n)), device_id_type=MESH)

    def y_copy(side, off):
        src, dst, to = (face_hi, edge_lo.at[pg], ty + 1) if side == 0 else (face_lo, edge_hi.at[pg], ty - 1)
        return pltpu.make_async_remote_copy(
            src, dst, y_send.at[side, off], y_recv.at[side, off],
            device_id=(tx, to, lax.rem(pg + off, pg_n)), device_id_type=MESH)

    sides = ((x_copy, 0, has_xh, has_xl), (x_copy, 1, has_xl, has_xh),
             (y_copy, 0, has_yh, has_yl), (y_copy, 1, has_yl, has_yh))
    for copy, side, sends, _ in sides:
        @pl.when(sends)
        def _():
            for off in range(pg_n):
                copy(side, off).start()
    for q in range(QUARTERS):
        for off in range(1, pg_n):
            mode_copy(off, q).start()
    wide[pl.ds(1, nx), pg] = own_ref[...]
    pairs_b[...] = jnp.zeros_like(pairs_b)
    adj_copy.wait()

    def turn_basis(i, carry):
        for more in range(4):
            k = i * 4 + more
            for c in range(3):
                adj_flat[pl.ds(c * nx * adj_n + k, nx, stride=adj_n), :] = adj_raw[k, c].astype(F32)
        return carry

    lax.fori_loop(0, adj_n // 4, turn_basis, 0)

    def arrived(sides):
        for copy, side, _, gets in sides:
            @pl.when(gets)
            def _():
                for off in range(pg_n):
                    copy(side, off).wait_recv()

    arrived((sides[0], sides[2], sides[3]))
    for off in range(1, pg_n):
        mode_copy(off, 0).wait_recv()

    place = lax.rem(lane, CZ)
    chunk_j = CHUNK // rows_n
    chunks = pg_n * own_n // chunk_j
    per_chunk = ty_n // chunks
    _, _, k_width, width = stage.shape

    def grads(x, carry):
        for p in range(pg_n):
            rows = pl.ds(p * own_n // blk, own_n // blk)
            for c in range(3):
                u = wide[x + 1, p, c].astype(F32)
                us[x, c, rows] = u.reshape(own_n // blk, blk, lanes)
                gx = wide[x + 2, p, c].astype(F32) - wide[x, p, c].astype(F32)
                e_hi = pltpu.roll(edge_hi[p, c].astype(F32), lanes - CZ - x * CZ, 1)
                e_lo = pltpu.roll(edge_lo[p, c].astype(F32), lax.rem(lanes - x * CZ, lanes), 1)
                up = jnp.where(lane >= lanes - CZ, e_hi, pltpu.roll(u, lanes - CZ, 1))
                down = jnp.where(lane < CZ, e_lo, pltpu.roll(u, CZ, 1))
                gy = up - down
                upper = jnp.where(place == CZ - 1, pltpu.roll(u, CZ - 1, 1), pltpu.roll(u, lanes - 1, 1))
                lower = jnp.where(place == 0, pltpu.roll(u, lanes - CZ + 1, 1), pltpu.roll(u, 1, 1))
                gz = upper - lower
                for d, g in enumerate((gx, gy, gz)):
                    g = (g * 0.5).astype(BF16).astype(F32)
                    gs[x, d * 3 + c, rows] = g.reshape(own_n // blk, blk, lanes)
        for b in range(per_group):
            s = order_ref[pg * per_group + b]
            for d in range(3):
                row_us[x, d, b] = us[x, d, s]
            for i in range(9):
                row_gs[x, i, b] = gs[x, i, s]
        return carry

    def projected(pairs, x0, piece=None):
        parts_of = 6 // PIECES
        ks = range(6) if piece is None else range(piece * parts_of, (piece + 1) * parts_of)
        basis = jnp.concatenate(
            [adj_flat[pl.ds(pl.multiple_of((k // 2 * nx + x0 + k % 2) * adj_n, adj_n), adj_n), :]
             for k in ks], 1).astype(BF16)
        return lax.dot_general(
            basis, pairs[:, ks[0] * lanes:(ks[-1] + 1) * lanes], (((1,), (1,)), ((), ())),
            preferred_element_type=F32)

    def form(pairs, x0, ch, other, y0):
        made = jnp.zeros((adj_n, CHUNK), F32)
        for xx in range(2):
            x = x0 + xx
            row_u = [[row_us[x, d, b] for b in range(per_group)] for d in range(3)]
            row_g = [[row_gs[x, i, b] for b in range(per_group)] for i in range(9)]
            for jj in range(chunk_j):
                at = xx * chunk_j + jj
                for piece in range(PIECES):
                    if at == piece * 2 * chunk_j // PIECES:
                        made = made + projected(other, y0, piece)
                jb, jr = ch * (chunk_j // blk) + jj // blk, pl.ds(jj % blk, 1)
                ju = [jnp.broadcast_to(us[x, d, jb, jr], (blk, lanes)) for d in range(3)]
                jg = [jnp.broadcast_to(gs[x, i, jb, jr], (blk, lanes)) for i in range(9)]
                for c in range(3):
                    both = []
                    for b in range(per_group):
                        total = row_u[0][b] * jg[c] + ju[0] * row_g[c][b]
                        for d in range(1, 3):
                            total = total + row_u[d][b] * jg[d * 3 + c]
                            total = total + ju[d] * row_g[d * 3 + c][b]
                        both.append(total)
                    pairs[pl.ds(jj * rows_n, rows_n), pl.ds((2 * c + xx) * lanes, lanes)] = (
                        jnp.concatenate(both, 0).astype(BF16))
        return made

    def part_copy(off):
        to = lax.rem(me + off, group_n)
        to_x, to_y = to // ty_n, lax.rem(to, ty_n)
        return pltpu.make_async_remote_copy(
            stage.at[to_y, to_x], parts.at[me], part_send.at[off], part_recv.at[off],
            device_id=(to_x, to_y, pg), device_id_type=MESH)

    def step(index, carry):
        turn, q = index // QUARTERS, lax.rem(index, QUARTERS)
        ch = lax.rem(ty // per_chunk + 1 + turn, chunks)

        @pl.when(turn == 0)
        def _():
            @pl.when(q < QUARTERS - 1)
            def _():
                for off in range(1, pg_n):
                    mode_copy(off, q + 1).wait_recv()

            @pl.when(q == QUARTERS - 1)
            def _():
                arrived((sides[1],))

            lax.fori_loop(0, quarter, lambda i, c: grads(q * quarter + i, c), 0, unroll=True)

        def two(i, carry):
            x0 = q * quarter + 4 * i
            last = form(pairs_a, x0, ch, pairs_b, lax.rem(x0 + nx - 2, nx))
            acc[...] = jnp.where(x0 == 0, 0.0, acc[...] + last)
            acc[...] += form(pairs_b, x0 + 2, ch, pairs_a, x0)
            return carry

        if quarter == 4:
            two(0, 0)
        else:
            lax.fori_loop(0, quarter // 4, two, 0)

        @pl.when(q == QUARTERS - 1)
        def _():
            block = (acc[...] + projected(pairs_b, nx - 2)) * weight
            for i in range(per_chunk):
                to_y = ch * per_chunk + i
                for t in range(tx_n):
                    stage[to_y, t] = block[
                        t * k_width:(t + 1) * k_width, i * width:(i + 1) * width].astype(stage.dtype)
                    to = t * ty_n + to_y

                    @pl.when(to != me)
                    def _():
                        part_copy(lax.rem(to - me + group_n, group_n)).start()
        return carry

    lax.fori_loop(0, chunks * QUARTERS, step, 0)
    parts[me] = stage[ty, tx]

    for q in range(QUARTERS):
        for off in range(1, pg_n):
            mode_copy(off, q).wait_send()
    for copy, side, sends, _ in sides:
        @pl.when(sends)
        def _():
            for off in range(pg_n):
                copy(side, off).wait_send()
    for off in range(1, group_n):
        part_copy(off).wait()
    result = parts[0].astype(F32)
    for source in range(1, group_n):
        result = result + parts[source].astype(F32)
    out_ref[...] = result


def shards(direct_modes, adjoint_modes, block_order):
    tx_n, ty_n, pg_n = lax.axis_size("tx"), lax.axis_size("ty"), lax.axis_size("pg")
    own_n, _, nx, lanes = direct_modes.shape
    adj_n = adjoint_modes.shape[0]
    mode_n = own_n * pg_n
    weight = 1.0 / math.sqrt(3.0 * nx * tx_n * lanes * ty_n)
    j_width, k_width = mode_n // ty_n, adj_n // tx_n
    width = j_width * own_n
    blk = mode_n // NBLK
    vmem = pl.BlockSpec(memory_space=pltpu.VMEM)
    dma = pltpu.SemaphoreType.DMA
    summed = pl.pallas_call(
        functools.partial(kernel, tx_n, ty_n, pg_n, weight),
        out_shape=jax.ShapeDtypeStruct((k_width, width), F32),
        in_specs=[pl.BlockSpec(memory_space=pltpu.SMEM)] + [pl.BlockSpec(memory_space=pl.ANY)] * 2,
        out_specs=vmem,
        scratch_shapes=[
            pltpu.VMEM((own_n, 3, nx, lanes), BF16),
            dma,
            pltpu.VMEM((nx * 3 * own_n, lanes), F32),
            pltpu.VMEM((nx, 3, own_n, lanes), BF16),
            pltpu.VMEM((adj_n, 3, nx, lanes), BF16),
            pltpu.VMEM((3 * nx * adj_n, lanes), F32),
            dma,
            pltpu.VMEM((nx + 2, pg_n, 3, own_n, lanes), BF16),
            pltpu.VMEM((3, own_n, lanes), BF16),
            pltpu.VMEM((3, own_n, lanes), BF16),
            pltpu.VMEM((pg_n, 3, own_n, lanes), BF16),
            pltpu.VMEM((pg_n, 3, own_n, lanes), BF16),
            pltpu.VMEM((nx, 3, NBLK, blk, lanes), F32),
            pltpu.VMEM((nx, 9, NBLK, blk, lanes), F32),
            pltpu.VMEM((nx, 3, NBLK // pg_n, blk, lanes), F32),
            pltpu.VMEM((nx, 9, NBLK // pg_n, blk, lanes), F32),
            pltpu.VMEM((CHUNK, 6 * lanes), BF16),
            pltpu.VMEM((CHUNK, 6 * lanes), BF16),
            pltpu.VMEM((adj_n, CHUNK), F32),
            pltpu.VMEM((ty_n, tx_n, k_width, width), BF16),
            pltpu.VMEM((tx_n * ty_n, k_width, width), BF16),
            dma((pg_n, QUARTERS)), dma((pg_n, QUARTERS)),
            dma((2, pg_n)), dma((2, pg_n)),
            dma((2, pg_n)), dma((2, pg_n)),
            dma((tx_n * ty_n,)), dma((tx_n * ty_n,)),
        ],
        compiler_params=pltpu.CompilerParams(
            collective_id=0, has_side_effects=True, vmem_limit_bytes=60 * 2**20),
    )(block_order, direct_modes, adjoint_modes)
    return jnp.transpose(summed.reshape(k_width, j_width, own_n), (2, 1, 0))


def solution(mesh):
    placed = (P("pg", None, "tx", "ty"), P(None, None, "tx", "ty"), P())
    return jax.shard_map(
        shards, mesh=mesh, in_specs=placed, out_specs=P("pg", "ty", "tx"), check_vma=False
    )
```
